32 devices in a mesh: bx: 8 (over z, x), by: 4 (over y, core).
Axes of the slice: x: 2, y: 2, z: 4, core: 2. Of those that a mesh axis runs over, the one named last changes fastest.
Arguments:
- box_map: float32 [8, 4, 256, 256], P('bx', 'by'), as said below
- box_load: float32 [8, 4, 64, 256], P('bx', 'by'), may hold values from -6 to 6
- box_order: int32 [8, 4, 256], P('bx', 'by'), may hold values from 0 to 255, each once within a row
- incoming: float32 [8, 4, 64, 128], P('bx', 'by'), may hold values from -54 to 54
- edge_map: float32 [8, 4, 256, 128], P('bx', 'by'), may hold values from -0.375 to 0.375
- edge_load: float32 [8, 4, 64, 128], P('bx', 'by'), may hold values from -6 to 6
Outputs:
- top_map: float32 [8, 4, 512, 128], P('bx', 'by')
- top_load: float32 [8, 4, 64, 128], P('bx', 'by')
- box_incoming: float32 [8, 4, 64, 256], P('bx', 'by')
- edge_values: float32 [8, 4, 64, 128], P('bx', 'by')
The draws below stay inside these ranges and needn't reach their ends.
Inputs may be any that keep to these rules, and one draw needn't show every extreme that they name: Each row of box_order holds every number from 0 to 255 once. Every box_map[i, j] has spectral norm at most 0.7.
All inputs are finite; a program needn't handle non-finite values.
Results may differ from the reference program's by a relative error of at most 0.0001.
Values sent between devices are 32-bit elements; how exact they have to be, the bound alone decides.
No kernel may reach another device: no remote copies, remote signals or barrier semaphores. Data moves between devices by JAX's collectives and lax.ppermute only.
A program may use at most 64 MiB of HBM per device.

```python
import jax
import jax.numpy as jnp
from jax import lax

SIDE = 32
NRHS = 64
BOUNDARY = 256
GX = 8
GY = 4
INNER = 128


def draw_box_map(key, part):
    box_count = GX * GY
    normal_key = jax.random.fold_in(key, 11)
    column_key = jax.random.fold_in(key, 12)
    gaussian = jax.random.normal(normal_key, (box_count, BOUNDARY, BOUNDARY), jnp.float32)
    orthogonal, triangle = jnp.linalg.qr(gaussian)
    column_scale = jax.random.uniform(column_key, (box_count, 1, BOUNDARY), jnp.float32, 0.5, 1.0)
    values = 0.7 * orthogonal * column_scale
    return values.reshape(GX, GY, BOUNDARY, BOUNDARY)


def draw_incoming(key, part):
    normal_key = jax.random.fold_in(key, 21)
    x_rise = 1.0 + 2.0 * jnp.arange(GX, dtype=jnp.float32) / (GX - 1)
    y_rise = 1.0 + 2.0 * jnp.arange(GY, dtype=jnp.float32) / (GY - 1)
    rise = x_rise[:, None, None, None] * y_rise[None, :, None, None]
    noise = jnp.clip(jax.random.normal(normal_key, (GX, GY, NRHS, 4 * SIDE), jnp.float32), -5.0, 5.0)
    values = rise * noise
    return values


def shard_levels(own_key, shape, cuts, low, top_value):
    level, own = 1.0, jax.random.fold_in(own_key, 6)
    for dim, shards_of in cuts:
        heights = jnp.exp(jax.random.uniform(jax.random.fold_in(own, dim), (shards_of,), jnp.float32, low / len(cuts), top_value / len(cuts)))
        level = level * jnp.repeat(heights, shape[dim] // shards_of).reshape([-1 if axis == dim else 1 for axis in range(len(shape))])
    return level


def scatter_about(key, extent, deviation, limit, cuts=(), held_as=jnp.bfloat16):
    result = jax.random.normal(key, extent, jnp.float32) * deviation
    if len(cuts) > 0:
        result = shard_levels(key, extent, cuts, -0.22, 0.18) * result
    return jnp.clip(result, min=-limit, max=limit).astype(held_as)


def setup_inputs(seed: int = 0) -> dict:
    keys = jax.random.split(jax.random.key(seed), 7)
    return {
        "box_map": draw_box_map(jax.random.fold_in(keys[6], 71), 0),
        "box_load": scatter_about(keys[1], (GX, GY, NRHS, BOUNDARY), 1.0, 6.0, ((0, 8), (1, 4)), jnp.float32),
        "box_order": jax.vmap(lambda own: jax.random.permutation(own, BOUNDARY))(jax.random.split(keys[2], GX * GY)).reshape((GX, GY, BOUNDARY)).astype(jnp.int32),
        "incoming": draw_incoming(jax.random.fold_in(keys[6], 71), 0),
        "edge_map": scatter_about(keys[4], (GX, GY, BOUNDARY, INNER), BOUNDARY ** -0.5, 0.375, ((0, 8), (1, 4)), jnp.float32),
        "edge_load": scatter_about(keys[5], (GX, GY, NRHS, INNER), 1.0, 6.0, ((0, 8), (1, 4)), jnp.float32),
    }


ALPHA_ORDER = ((0, 2, 3, 1), (0, 3, 2, 1))
BETA_ORDER = ((1, 2, 3, 0), (1, 3, 2, 0))
MACRO_ORDER = (0, 1, 3, 4, 2, 5)

def matmul(first, second):
    return jnp.dot(first.astype(jnp.float32), second.astype(jnp.float32), precision=lax.Precision.HIGHEST, preferred_element_type=jnp.float32)

def block_index(blocks, breadth):
    return jnp.concatenate([jnp.arange(breadth, dtype=jnp.int32) + number * breadth for number in blocks])

def canonical_blocks(order):
    return tuple((order.index(number) for number in range(4)))

def interface_terms(alpha_outer, alpha_inner, alpha_free, beta_outer, beta_inner, beta_free):
    inner_size = alpha_inner.shape[0]
    kernel = jnp.eye(inner_size, dtype=jnp.float32) - matmul(beta_inner, alpha_inner)
    inverse = jnp.linalg.inv(kernel)
    alpha_from_alpha = matmul(alpha_outer, inverse)
    alpha_from_beta = -matmul(matmul(beta_outer, alpha_inner), inverse)
    alpha_source = matmul(alpha_free - matmul(beta_free, alpha_inner), inverse)
    beta_from_alpha = -matmul(alpha_from_alpha, beta_inner)
    beta_from_beta = beta_outer - matmul(alpha_from_beta, beta_inner)
    beta_source = beta_free - matmul(alpha_source, beta_inner)
    return (alpha_from_alpha, alpha_from_beta, alpha_source, beta_from_alpha, beta_from_beta, beta_source)

def full_merge(alpha_map, alpha_load, beta_map, beta_load, outer):
    terms = interface_terms(alpha_map[:outer, outer:], alpha_map[outer:, outer:], alpha_load[:, outer:], beta_map[:outer, outer:], beta_map[outer:, outer:], beta_load[:, outer:])
    alpha_from_alpha, alpha_from_beta, alpha_source, beta_from_alpha, beta_from_beta, beta_source = terms
    alpha_back = alpha_map[outer:, :outer]
    beta_back = beta_map[outer:, :outer]
    upper = jnp.concatenate([alpha_map[:outer, :outer] - matmul(beta_from_alpha, alpha_back), -matmul(alpha_from_alpha, beta_back)], axis=1)
    lower = jnp.concatenate([-matmul(beta_from_beta, alpha_back), beta_map[:outer, :outer] - matmul(alpha_from_beta, beta_back)], axis=1)
    merged = jnp.concatenate([upper, lower], axis=0)
    merged_load = jnp.concatenate([alpha_load[:, :outer] - matmul(beta_source, alpha_back), beta_load[:, :outer] - matmul(alpha_source, beta_back)], axis=1)
    return (merged, merged_load, terms)

def interface_values(terms, alpha_in, beta_in):
    alpha_from_alpha, alpha_from_beta, alpha_source, beta_from_alpha, beta_from_beta, beta_source = terms
    alpha_value = matmul(alpha_in, alpha_from_alpha) + matmul(beta_in, alpha_from_beta) + alpha_source
    beta_value = matmul(alpha_in, beta_from_alpha) + matmul(beta_in, beta_from_beta) + beta_source
    return (alpha_value, beta_value)

def solve_group(group):
    maps, loads, orders, incoming, edge_map, edge_load = group
    breadth = 2 * SIDE
    macros = []
    for y_parity in range(2):
        roles = []
        for x_parity, table in ((0, ALPHA_ORDER), (1, BETA_ORDER)):
            picked = orders[x_parity, y_parity][block_index(table[y_parity], breadth)]
            single = maps[x_parity, y_parity]
            roles.append((single[picked][:, picked], loads[x_parity, y_parity][:, picked]))
        merged, merged_load, terms = full_merge(roles[0][0], roles[0][1], roles[1][0], roles[1][1], 3 * breadth)
        macro_index = block_index(MACRO_ORDER, breadth)
        macros.append((merged[macro_index][:, macro_index], merged_load[:, macro_index], terms))
    outer = 4 * breadth
    whole_map, whole_load, top_terms = full_merge(macros[0][0], macros[0][1], macros[1][0], macros[1][1], outer)
    outside = [jnp.concatenate([incoming[0, y_parity], incoming[1, y_parity]], axis=1) for y_parity in range(2)]
    bottom_value, upper_value = interface_values(top_terms, outside[0], outside[1])
    inside = [-upper_value, -bottom_value]
    results = {}
    for y_parity in range(2):
        alpha_in = jnp.concatenate([outside[y_parity][:, :2 * breadth], inside[y_parity][:, :breadth]], axis=1)
        beta_in = jnp.concatenate([outside[y_parity][:, 2 * breadth:], inside[y_parity][:, breadth:]], axis=1)
        alpha_value, beta_value = interface_values(macros[y_parity][2], alpha_in, beta_in)
        full_values = (jnp.concatenate([alpha_in, -beta_value], axis=1), jnp.concatenate([beta_in, -alpha_value], axis=1))
        for x_parity, table in ((0, ALPHA_ORDER), (1, BETA_ORDER)):
            canonical = full_values[x_parity][:, block_index(canonical_blocks(table[y_parity]), breadth)]
            start = (2 * y_parity + x_parity) * 2 * breadth
            edges = matmul(canonical, edge_map[x_parity, y_parity]) + edge_load[x_parity, y_parity]
            results[x_parity, y_parity] = (whole_map[:, start:start + 2 * breadth], whole_load[:, start:start + 2 * breadth], canonical, edges)
    outputs = []
    for member in range(4):
        outputs.append(jnp.stack([jnp.stack([results[x_parity, y_parity][member] for y_parity in range(2)]) for x_parity in range(2)]))
    return (outputs[0], outputs[1], outputs[2], outputs[3])

def to_groups(values_in):
    tail_shape = values_in.shape[2:]
    shaped = values_in.reshape((GX // 2, 2, GY // 2, 2) + tail_shape)
    order = (0, 2, 1, 3) + tuple(range(4, 4 + len(tail_shape)))
    return shaped.transpose(order).reshape((GX // 2 * (GY // 2), 2, 2) + tail_shape)

def from_groups(values_in):
    tail_shape = values_in.shape[3:]
    shaped = values_in.reshape((GX // 2, GY // 2, 2, 2) + tail_shape)
    order = (0, 2, 1, 3) + tuple(range(4, 4 + len(tail_shape)))
    return shaped.transpose(order).reshape((GX, GY) + tail_shape)

def reference(box_map, box_load, box_order, incoming, edge_map, edge_load):
    power = lax.optimization_barrier(jnp.sum(incoming * incoming, axis=(0, 1, 3)))
    factor = 1.0 / jnp.sqrt(power / (GX * GY * 4 * SIDE) + 1e-06)
    scaled = incoming * factor[None, None, :, None]
    grouped = (to_groups(box_map), to_groups(box_load), to_groups(box_order), to_groups(scaled), to_groups(edge_map), to_groups(edge_load))
    top_map, top_load, box_incoming, edge_values = lax.map(solve_group, grouped)
    return (from_groups(top_map), from_groups(top_load), from_groups(box_incoming), from_groups(edge_values))
```

```python
import functools

import jax
import jax.numpy as jnp
from jax import lax
from jax.experimental import pallas as pl
from jax.experimental.pallas import tpu as pltpu
from jax.sharding import PartitionSpec as P

VMEM = pl.BlockSpec(memory_space=pltpu.VMEM)
DOUBLINGS = 5


def swapped(block, axis, apart):
    count = lax.axis_size(axis)
    route = []
    for low in range(count):
        high = low | 1 << apart
        if high != low and high < count:
            route += [(low, high), (high, low)]
    return lax.ppermute(block, axis, route)


def dot(first, second):
    return jnp.dot(
        first, second, precision=lax.Precision.HIGH, preferred_element_type=jnp.float32
    )


def dot_one(first, second):
    return jnp.dot(first, second, preferred_element_type=jnp.float32)


def pieces(value):
    high = value.astype(jnp.bfloat16)
    rest = value - high.astype(jnp.float32)
    middle = rest.astype(jnp.bfloat16)
    low = (rest - middle.astype(jnp.float32)).astype(jnp.bfloat16)
    return high, middle, low


def own_parities():
    return lax.axis_index("bx") % 2, lax.axis_index("by") % 2


def permute_kernel(map_ref, load_ref, order_ref, incoming_ref, c0_ref, c1_ref, g0_ref, side_ref, power_ref):
    size = map_ref.shape[0]
    b = size // 4
    x_parity, y_parity = own_parities()
    order = order_ref[...]
    west, east, south, north = (order[:, n * b : (n + 1) * b] for n in range(4))
    outside = jnp.where(x_parity == 0, west, east)
    inside = jnp.where(x_parity == 0, east, west)
    first = jnp.where(y_parity == 0, south, north)
    second = jnp.where(y_parity == 0, north, south)
    picked = jnp.concatenate([outside, first, inside, second], axis=1)
    rows = lax.broadcasted_iota(jnp.int32, (size, size), 0)
    hot = jnp.where(rows == picked, 1.0, 0.0)
    hot_t = hot.T
    hot_rows = jnp.concatenate(
        [hot_t[: 2 * b], hot_t[3 * b :], hot_t[2 * b : 3 * b]], axis=0
    ).astype(jnp.bfloat16)
    hot = hot.astype(jnp.bfloat16)
    stacked = jnp.concatenate([map_ref[...], load_ref[...]], axis=0)
    by_column = [dot_one(piece, hot) for piece in pieces(stacked)]
    role_load = by_column[0][size:] + by_column[1][size:] + by_column[2][size:]
    by_row = [dot_one(hot_rows, part[:size].astype(jnp.bfloat16)) for part in by_column]
    role_map = by_row[0] + by_row[1] + by_row[2]
    c0_ref[...] = role_map[:, : 2 * b]
    c1_ref[...] = role_map[:, 2 * b :]
    g0_ref[...] = role_load[:, : 2 * b]
    count = load_ref.shape[0]
    raw = incoming_ref[...]
    side_ref[:count] = role_load[:, 2 * b :]
    side_ref[count:] = raw
    own_power = jnp.sum(raw * raw, axis=1, keepdims=True)
    at = lax.broadcasted_iota(jnp.int32, (count, 2 * b), 0)
    lane = lax.broadcasted_iota(jnp.int32, (count, 2 * b), 1)
    row = jnp.sum(jnp.where(at == lane, own_power, 0.0), axis=0, keepdims=True)
    power_ref[...] = jnp.broadcast_to(row, power_ref.shape)


def first_kernel(c0_ref, c1_ref, g0_ref, side_ref, f1_ref, fside_ref, p0_ref, send_ref, pl0_ref, z_ref):
    b = c0_ref.shape[1] // 2
    e = 3 * b
    count = g0_ref.shape[0]
    near, far = c1_ref[:, :b], f1_ref[:, :b]
    near_load, far_load = side_ref[:count], fside_ref[:count]
    a_cc, b_dd = near[e:], far[e:]
    both = dot(a_cc, f1_ref[e:])
    power = both[:, :b]
    right = jnp.concatenate([c0_ref[e:], c1_ref[e:, b:], both[:, b:]], axis=1)
    at = lax.broadcasted_iota(jnp.int32, (b, b), 0)
    lane = lax.broadcasted_iota(jnp.int32, (b, b), 1)
    z = jnp.where(at == lane, 1.0, 0.0) + power
    right = right + dot(power, right)
    for _ in range(DOUBLINGS - 1):
        power = dot(power, power)
        right = right + dot(power, right)
        z = z + dot(z, power)
    z_ref[...] = z
    back = dot(b_dd, right)
    t_part = jnp.concatenate(
        [back[:, :e], -(back[:, e:] + f1_ref[e:, b:])], axis=1
    )
    q_part = jnp.concatenate([-right[:, :e], right[:, e:]], axis=1)
    near_rows = dot(jnp.concatenate([near[:e], near_load[:, :b]], axis=0), t_part)
    far_rows = dot(jnp.concatenate([far[:e], far_load[:, :b]], axis=0), q_part)
    w = 2 * b
    p0_ref[:w] = near_rows[:w, :w] + c0_ref[:w]
    p0_ref[w : 2 * w] = far_rows[:w, :w]
    p0_ref[2 * w : 2 * w + b] = near_rows[w:e, :w] + c0_ref[w:e]
    p0_ref[2 * w + b : 3 * w] = far_rows[w:e, :w]
    near_y2 = jnp.concatenate([c1_ref[:e, b:], jnp.zeros((e, b), jnp.float32)], axis=1)
    far_y2 = jnp.concatenate([jnp.zeros((e, b), jnp.float32), f1_ref[:e, b:]], axis=1)
    send_ref[:w] = near_rows[:w, w:] + near_y2[:w]
    send_ref[w : 2 * w] = far_rows[:w, w:] + far_y2[:w]
    send_ref[2 * w : 2 * w + b] = near_rows[w:e, w:] + near_y2[w:]
    send_ref[2 * w + b : 3 * w] = far_rows[w:e, w:] + far_y2[w:]
    both_load = near_rows[e:] + far_rows[e:]
    pl0_ref[...] = g0_ref[...] + both_load[:, :w]
    send_ref[3 * w : 3 * w + count] = both_load[:, w:] + jnp.concatenate(
        [near_load[:, b:], far_load[:, b:]], axis=1
    )
    send_ref[3 * w + count : 3 * w + 2 * count] = side_ref[count:]
    send_ref[3 * w + 2 * count :] = fside_ref[count:]


def second_kernel(
    box_total, p0_ref, pl0_ref, own_ref, far_ref, c1_ref, f1_ref, side_ref, fside_ref, z_ref,
    power_ref, edge_ref, edge_load_ref, top_ref, top_load_ref, box_ref, values_ref
):
    w = p0_ref.shape[1]
    b = w // 2
    e = 3 * b
    count = pl0_ref.shape[0]
    x_parity, y_parity = own_parities()
    a_cc, b_dd = own_ref[2 * w : 3 * w], far_ref[2 * w : 3 * w]
    at = lax.broadcasted_iota(jnp.int32, (count, w), 0)
    lane = lax.broadcasted_iota(jnp.int32, (count, w), 1)
    total = jnp.sum(jnp.where(at == lane, power_ref[0:1], 0.0), axis=1, keepdims=True)
    factor = 1.0 / jnp.sqrt(total / (box_total * w) + 1e-06)
    near_inc = own_ref[3 * w + count : 3 * w + 2 * count] * factor
    next_inc = own_ref[3 * w + 2 * count : 3 * w + 3 * count] * factor
    far_incs = jnp.concatenate(
        [far_ref[3 * w + count : 3 * w + 2 * count], far_ref[3 * w + 2 * count : 3 * w + 3 * count]], axis=1
    ) * factor
    a_out = dot(jnp.concatenate([near_inc, next_inc], axis=1), own_ref[: 2 * w]) + own_ref[3 * w : 3 * w + count]
    b_out = dot(far_incs, far_ref[: 2 * w]) + far_ref[3 * w : 3 * w + count]
    left = b_out - dot(a_out, b_dd)
    power = dot(a_cc, b_dd)
    right = p0_ref[2 * w :]
    right = right + dot(power, right)
    left = left + dot(left, power)
    for _ in range(DOUBLINGS - 1):
        power = dot(power, power)
        right = right + dot(power, right)
        left = left + dot(left, power)
    back = dot(b_dd, right)
    near_rows = p0_ref[: 2 * w] + dot(own_ref[: 2 * w], back)
    far_rows = -dot(far_ref[: 2 * w], right)
    swap = x_parity
    near_at = pl.multiple_of(y_parity * 2 * w, w)
    far_at = pl.multiple_of((1 - y_parity) * 2 * w, w)
    top_ref[pl.ds(pl.multiple_of(near_at + swap * w, w), w)] = near_rows[:w]
    top_ref[pl.ds(pl.multiple_of(near_at + (1 - swap) * w, w), w)] = near_rows[w:]
    top_ref[pl.ds(pl.multiple_of(far_at + swap * w, w), w)] = far_rows[:w]
    top_ref[pl.ds(pl.multiple_of(far_at + (1 - swap) * w, w), w)] = far_rows[w:]
    top_load_ref[...] = (
        pl0_ref[...]
        + dot(own_ref[3 * w : 3 * w + count], back)
        - dot(far_ref[3 * w : 3 * w + count], right)
    )
    near_y2, next_y2 = -left[:, :b], -left[:, b:]
    near_in = jnp.concatenate([near_inc, near_y2], axis=1)
    next_in = jnp.concatenate([next_inc, next_y2], axis=1)
    a_out = dot(near_in, c1_ref[:e, :b]) + side_ref[:count, :b]
    b_out = dot(next_in, f1_ref[:e, :b]) + fside_ref[:count, :b]
    inside = -dot(b_out - dot(a_out, f1_ref[e:, :b]), z_ref[...])
    outside = near_inc[:, :b]
    first = near_inc[:, b:]
    x_sides = jnp.where(
        x_parity == 0,
        jnp.concatenate([outside, inside], axis=1),
        jnp.concatenate([inside, outside], axis=1),
    )
    y_sides = jnp.where(
        y_parity == 0,
        jnp.concatenate([first, near_y2], axis=1),
        jnp.concatenate([near_y2, first], axis=1),
    )
    box_ref[:, :w] = x_sides
    box_ref[:, w:] = y_sides
    values_ref[...] = dot(x_sides, edge_ref[:w]) + dot(y_sides, edge_ref[w:]) + edge_load_ref[...]


def call(kernel, outs, *operands):
    return pl.pallas_call(
        kernel,
        out_shape=[jax.ShapeDtypeStruct(shape, jnp.float32) for shape in outs],
        in_specs=[VMEM] * len(operands),
        out_specs=[VMEM] * len(outs),
    )(*operands)


def body(box_map, box_load, box_order, incoming, edge_map, edge_load):
    size = box_map.shape[2]
    w = size // 2
    b = size // 4
    count = box_load.shape[2]
    wide, high = lax.axis_size("bx"), lax.axis_size("by")
    c0, c1, g0, side, power = call(
        permute_kernel,
        [(size, w), (size, w), (count, w), (2 * count, w), (8, w)],
        box_map[0, 0], box_load[0, 0], box_order[0], incoming[0, 0],
    )
    for axis, extent in (("bx", wide), ("by", high)):
        for apart in range(1, extent.bit_length() - 1):
            power = power + swapped(power, axis, apart)
    power = power + swapped(power, "bx", 0)
    power = power + swapped(power, "by", 0)
    f1 = swapped(c1, "bx", 0)
    fside = swapped(side, "bx", 0)
    p0, send, pl0, z = call(
        first_kernel,
        [(3 * w, w), (3 * w + 3 * count, w), (count, w), (b, b)],
        c0, c1, g0, side, f1, fside,
    )
    far = swapped(send, "by", 0)
    top, top_load, box, values = call(
        functools.partial(second_kernel, wide * high),
        [(4 * w, w), (count, w), (count, size), (count, w)],
        p0, pl0, send, far, c1, f1, side, fside, z, power, edge_map[0, 0], edge_load[0, 0],
    )
    return top[None, None], top_load[None, None], box[None, None], values[None, None]


def solution(mesh):
    spec = P("bx", "by", None, None)
    return jax.shard_map(
        body,
        mesh=mesh,
        in_specs=(spec, spec, P("bx", "by", None), spec, spec, spec),
        out_specs=(spec,) * 4,
        check_vma=False,
    )
```

```python
import functools

import jax
import jax.numpy as jnp
from jax import lax
from jax.experimental import pallas as pl
from jax.experimental.pallas import tpu as pltpu
from jax.sharding import PartitionSpec as P


VMEM = pl.BlockSpec(memory_space=pltpu.VMEM)
DOUBLINGS = 5


def swapped(block, axis, apart):
    count = lax.axis_size(axis)
    route = []
    for low in range(count):
        high = low | 1 << apart
        if high != low and high < count:
            route += [(low, high), (high, low)]
    return lax.ppermute(block, axis, route)


def dot(first, second):
    return jnp.dot(
        first, second, precision=lax.Precision.HIGH, preferred_element_type=jnp.float32
    )


def dot_one(first, second):
    return jnp.dot(first, second, preferred_element_type=jnp.float32)


def pieces(value):
    high = value.astype(jnp.bfloat16)
    rest = value - high.astype(jnp.float32)
    middle = rest.astype(jnp.bfloat16)
    low = (rest - middle.astype(jnp.float32)).astype(jnp.bfloat16)
    return high, middle, low


def own_parities():
    return lax.axis_index("bx") % 2, lax.axis_index("by") % 2


def permute_kernel(map_ref, load_ref, order_ref, c0_ref, c1_ref, g0_ref, g1_ref, all_ref, own_order_ref, sems):
    size = map_ref.shape[0]
    b = size // 4
    x_parity, y_parity = own_parities()
    order_copy = pltpu.make_async_copy(order_ref, own_order_ref, sems.at[0])
    map_copy = pltpu.make_async_copy(map_ref, all_ref.at[:size], sems.at[1])
    load_copy = pltpu.make_async_copy(load_ref, all_ref.at[size:], sems.at[2])
    for copy in (order_copy, map_copy, load_copy):
        copy.start()
    order_copy.wait()
    order = own_order_ref[...]
    west, east, south, north = (order[:, n * b : (n + 1) * b] for n in range(4))
    outside = jnp.where(x_parity == 0, west, east)
    inside = jnp.where(x_parity == 0, east, west)
    first = jnp.where(y_parity == 0, south, north)
    second = jnp.where(y_parity == 0, north, south)
    picked = jnp.concatenate([outside, first, inside, second], axis=1)
    rows = lax.broadcasted_iota(jnp.int32, (size, size), 0)
    hot = jnp.where(rows == picked, 1.0, 0.0)
    hot_t = hot.T
    hot_rows = jnp.concatenate(
        [hot_t[: 2 * b], hot_t[3 * b :], hot_t[2 * b : 3 * b]], axis=0
    ).astype(jnp.bfloat16)
    hot = hot.astype(jnp.bfloat16)
    map_copy.wait()
    load_copy.wait()
    by_column = [dot_one(piece, hot) for piece in pieces(all_ref[...])]
    role_load = by_column[0][size:] + by_column[1][size:] + by_column[2][size:]
    by_row = [dot_one(hot_rows, part[:size].astype(jnp.bfloat16)) for part in by_column]
    role_map = by_row[0] + by_row[1] + by_row[2]
    c0_ref[...] = role_map[:, : 2 * b]
    c1_ref[...] = role_map[:, 2 * b :]
    g0_ref[...] = role_load[:, : 2 * b]
    g1_ref[...] = role_load[:, 2 * b :]


def pair_power_kernel(inc_ref, next_ref, power_ref):
    count, w = inc_ref.shape
    own, other = inc_ref[...], next_ref[...]
    total = jnp.sum(own * own + other * other, axis=1, keepdims=True)
    at = lax.broadcasted_iota(jnp.int32, (count, w), 0)
    lane = lax.broadcasted_iota(jnp.int32, (count, w), 1)
    row = jnp.sum(jnp.where(at == lane, total, 0.0), axis=0, keepdims=True)
    power_ref[...] = jnp.broadcast_to(row, power_ref.shape)


def first_solve_kernel(c0_ref, c1_ref, f1_ref, t_ref, q_ref, z_ref):
    b = c0_ref.shape[1] // 2
    e = 3 * b
    a_cc, b_dd = c1_ref[e:, :b], f1_ref[e:, :b]
    both = dot(a_cc, f1_ref[e:])
    power = both[:, :b]
    right = jnp.concatenate([c0_ref[e:], c1_ref[e:, b:], both[:, b:]], axis=1)
    at = lax.broadcasted_iota(jnp.int32, (b, b), 0)
    lane = lax.broadcasted_iota(jnp.int32, (b, b), 1)
    z = jnp.where(at == lane, 1.0, 0.0) + power
    right = right + dot(power, right)
    for _ in range(DOUBLINGS - 1):
        power = dot(power, power)
        right = right + dot(power, right)
        z = z + dot(z, power)
    z_ref[...] = z
    back = dot(b_dd, right)
    t_ref[...] = jnp.concatenate([back[:, :e], -(back[:, e:] + f1_ref[e:, b:])], axis=1)
    q_ref[...] = jnp.concatenate([-right[:, :e], right[:, e:]], axis=1)


def first_merge_kernel(
    c0_ref, c1_ref, g0_ref, g1_ref, f1_ref, fg1_ref, inc_ref, next_ref, t_ref, q_ref,
    p0_ref, pl0_ref, send_ref
):
    w = c0_ref.shape[1]
    b = w // 2
    e = 3 * b
    count = g0_ref.shape[0]
    near_rows = dot(jnp.concatenate([c1_ref[:e, :b], g1_ref[:, :b]], axis=0), t_ref[...])
    far_rows = dot(jnp.concatenate([f1_ref[:e, :b], fg1_ref[:, :b]], axis=0), q_ref[...])
    p0_ref[:w] = near_rows[:w, :w] + c0_ref[:w]
    p0_ref[w : 2 * w] = far_rows[:w, :w]
    p0_ref[2 * w : 2 * w + b] = near_rows[w:e, :w] + c0_ref[w:e]
    p0_ref[2 * w + b :] = far_rows[w:e, :w]
    near_y2 = jnp.concatenate([c1_ref[:e, b:], jnp.zeros((e, b), jnp.float32)], axis=1)
    far_y2 = jnp.concatenate([jnp.zeros((e, b), jnp.float32), f1_ref[:e, b:]], axis=1)
    send_ref[:w] = near_rows[:w, w:] + near_y2[:w]
    send_ref[w : 2 * w] = far_rows[:w, w:] + far_y2[:w]
    send_ref[2 * w : 2 * w + b] = near_rows[w:e, w:] + near_y2[w:]
    send_ref[2 * w + b : 3 * w] = far_rows[w:e, w:] + far_y2[w:]
    both_load = near_rows[e:] + far_rows[e:]
    pl0_ref[...] = g0_ref[...] + both_load[:, :w]
    send_ref[3 * w : 3 * w + count] = both_load[:, w:] + jnp.concatenate(
        [g1_ref[:, b:], fg1_ref[:, b:]], axis=1
    )
    send_ref[3 * w + count : 3 * w + 2 * count] = inc_ref[...]
    send_ref[3 * w + 2 * count :] = next_ref[...]


def second_solve_kernel(p0_ref, own_ref, far_ref, right_ref, back_ref, left_ref):
    w = p0_ref.shape[1]
    count = (own_ref.shape[0] - 3 * w) // 3
    a_cc, b_dd = own_ref[2 * w : 3 * w], far_ref[2 * w : 3 * w]
    at = 3 * w + count
    own_incs = jnp.concatenate([own_ref[at : at + count], own_ref[at + count :]], axis=1)
    far_incs = jnp.concatenate([far_ref[at : at + count], far_ref[at + count :]], axis=1)
    a_out = jnp.concatenate([dot(own_incs, own_ref[: 2 * w]), own_ref[3 * w : at]], axis=0)
    b_out = jnp.concatenate([dot(far_incs, far_ref[: 2 * w]), far_ref[3 * w : at]], axis=0)
    left = b_out - dot(a_out, b_dd)
    power = dot(a_cc, b_dd)
    right = p0_ref[2 * w :]
    right = right + dot(power, right)
    left = left + dot(left, power)
    for _ in range(DOUBLINGS - 1):
        power = dot(power, power)
        right = right + dot(power, right)
        left = left + dot(left, power)
    right_ref[...] = right
    back_ref[...] = dot(b_dd, right)
    left_ref[...] = -left


def second_merge_kernel(
    p0_ref, pl0_ref, own_ref, far_ref, c1_ref, g1_ref, f1_ref, fg1_ref, inc_ref, next_ref, z_ref,
    right_ref, back_ref, left_ref, edge_ref, edge_load_ref, top_ref, top_load_ref, box_ref, values_ref,
    own_edge_ref, own_edge_load_ref, own_top_ref, own_top_load_ref, sems
):
    edge_copy = pltpu.make_async_copy(edge_ref, own_edge_ref, sems.at[0])
    edge_load_copy = pltpu.make_async_copy(edge_load_ref, own_edge_load_ref, sems.at[1])
    edge_copy.start()
    edge_load_copy.start()
    w = p0_ref.shape[1]
    b = w // 2
    e = 3 * b
    count = pl0_ref.shape[0]
    x_parity, y_parity = own_parities()
    near_rows = p0_ref[: 2 * w] + dot(own_ref[: 2 * w], back_ref[...])
    far_rows = -dot(far_ref[: 2 * w], right_ref[...])
    near_at = y_parity * 2 * w
    far_at = (1 - y_parity) * 2 * w
    for rows, start in ((near_rows, near_at), (far_rows, far_at)):
        own_top_ref[pl.ds(pl.multiple_of(start + x_parity * w, w), w)] = rows[:w]
        own_top_ref[pl.ds(pl.multiple_of(start + (1 - x_parity) * w, w), w)] = rows[w:]
    own_top_load_ref[...] = (
        pl0_ref[...]
        + dot(own_ref[3 * w : 3 * w + count], back_ref[...])
        - dot(far_ref[3 * w : 3 * w + count], right_ref[...])
    )
    top_copy = pltpu.make_async_copy(own_top_ref, top_ref, sems.at[2])
    top_load_copy = pltpu.make_async_copy(own_top_load_ref, top_load_ref, sems.at[3])
    top_copy.start()
    top_load_copy.start()
    none = jnp.zeros((count, w), jnp.float32)
    near_inc = jnp.concatenate([inc_ref[...], none], axis=0)
    next_inc = jnp.concatenate([next_ref[...], none], axis=0)
    near_y2 = left_ref[:, :b]
    near_in = jnp.concatenate([near_inc, near_y2], axis=1)
    next_in = jnp.concatenate([next_inc, left_ref[:, b:]], axis=1)
    a_out = dot(near_in, c1_ref[:e, :b]) + jnp.concatenate([none[:, :b], g1_ref[:, :b]], axis=0)
    b_out = dot(next_in, f1_ref[:e, :b]) + jnp.concatenate([none[:, :b], fg1_ref[:, :b]], axis=0)
    inside = -dot(b_out - dot(a_out, f1_ref[e:, :b]), z_ref[...])
    outside = near_inc[:, :b]
    first = near_inc[:, b:]
    x_sides = jnp.where(
        x_parity == 0,
        jnp.concatenate([outside, inside], axis=1),
        jnp.concatenate([inside, outside], axis=1),
    )
    y_sides = jnp.where(
        y_parity == 0,
        jnp.concatenate([first, near_y2], axis=1),
        jnp.concatenate([near_y2, first], axis=1),
    )
    box_ref[:, :w] = x_sides
    box_ref[:, w:] = y_sides
    edge_copy.wait()
    edge_load_copy.wait()
    values = dot(x_sides, own_edge_ref[:w]) + dot(y_sides, own_edge_ref[w:])
    values_ref[:count] = values[:count]
    values_ref[count:] = values[count:] + own_edge_load_ref[...]
    top_copy.wait()
    top_load_copy.wait()


def scale_kernel(box_total, box_ref, values_ref, power_ref, added_ref, out_box_ref, out_values_ref):
    count, w = out_values_ref.shape
    at = lax.broadcasted_iota(jnp.int32, (count, w), 0)
    lane = lax.broadcasted_iota(jnp.int32, (count, w), 1)
    power = power_ref[0:1] + added_ref[0:1]
    total = jnp.sum(jnp.where(at == lane, power, 0.0), axis=1, keepdims=True)
    factor = 1.0 / jnp.sqrt(total / (box_total * w) + 1e-06)
    out_box_ref[...] = box_ref[:count] * factor + box_ref[count:]
    out_values_ref[...] = values_ref[:count] * factor + values_ref[count:]


def call(kernel, outs, *operands, distant=(), scratch=()):
    away = pl.BlockSpec(memory_space=pl.ANY)
    placed = [
        operand if number in distant else pltpu.with_memory_space_constraint(operand, pltpu.VMEM)
        for number, operand in enumerate(operands)
    ]
    return pl.pallas_call(
        kernel,
        out_shape=[
            (pltpu.VMEM if place == "here" else pltpu.HBM)(shape, jnp.float32)
            for place, shape in outs
        ],
        in_specs=[away if number in distant else VMEM for number in range(len(operands))],
        out_specs=[away if place == "copied" else VMEM for place, shape in outs],
        scratch_shapes=list(scratch),
    )(*placed)


def body(box_map, box_load, box_order, incoming, edge_map, edge_load):
    size = box_map.shape[2]
    w = size // 2
    b = size // 4
    count = box_load.shape[2]
    wide, high = lax.axis_size("bx"), lax.axis_size("by")
    here, there, copied = "here", "there", "copied"
    own_inc = incoming[0, 0]
    next_inc = swapped(own_inc, "bx", 0)
    c0, c1, g0, g1 = call(
        permute_kernel,
        [(here, (size, w)), (here, (size, w)), (here, (count, w)), (here, (count, w))],
        box_map[0, 0], box_load[0, 0], box_order[0],
        distant=(0, 1, 2),
        scratch=[
            pltpu.VMEM((size + count, size), jnp.float32),
            pltpu.VMEM((1, size), jnp.int32),
            pltpu.SemaphoreType.DMA((3,)),
        ],
    )
    f1 = swapped(c1, "bx", 0)
    (power,) = call(pair_power_kernel, [(here, (8, w))], own_inc, next_inc)
    stages = [("by", apart) for apart in range(1, high.bit_length() - 1)]
    stages += [("bx", apart) for apart in range(1, wide.bit_length() - 1)]
    for axis, apart in stages:
        power = power + swapped(power, axis, apart)
    fg1 = swapped(g1, "bx", 0)
    added = swapped(power, "by", 0)
    t_part, q_part, z = call(
        first_solve_kernel,
        [(here, (b, size)), (here, (b, size)), (here, (b, b))],
        c0, c1, f1,
    )
    p0, pl0, own = call(
        first_merge_kernel,
        [(here, (3 * w, w)), (here, (count, w)), (here, (3 * w + 3 * count, w))],
        c0, c1, g0, g1, f1, fg1, own_inc, next_inc, t_part, q_part,
    )
    far = swapped(own, "by", 0)
    right, back, left = call(
        second_solve_kernel,
        [(here, (w, w)), (here, (w, w)), (here, (2 * count, w))],
        p0, own, far,
    )
    top, top_load, box, values = call(
        second_merge_kernel,
        [(copied, (4 * w, w)), (copied, (count, w)), (here, (2 * count, size)), (here, (2 * count, w))],
        p0, pl0, own, far, c1, g1, f1, fg1, own_inc, next_inc, z, right, back, left,
        edge_map[0, 0], edge_load[0, 0],
        distant=(14, 15),
        scratch=[
            pltpu.VMEM((size, w), jnp.float32),
            pltpu.VMEM((count, w), jnp.float32),
            pltpu.VMEM((4 * w, w), jnp.float32),
            pltpu.VMEM((count, w), jnp.float32),
            pltpu.SemaphoreType.DMA((4,)),
        ],
    )
    box, values = call(
        functools.partial(scale_kernel, wide * high),
        [(there, (count, size)), (there, (count, w))],
        box, values, power, added,
    )
    return top[None, None], top_load[None, None], box[None, None], values[None, None]


def solution(mesh):
    spec = P("bx", "by", None, None)

    return jax.shard_map(
        body,
        mesh=mesh,
        in_specs=(spec, spec, P("bx", "by", None), spec, spec, spec),
        out_specs=(spec,) * 4,
        check_vma=False,
    )
```
